512 devices in a mesh: gx: 16 (over x, y_lo, core), gy: 32 (over y_hi, z).
Axes of the slice: x: 4, y: 8 (y_hi: 4, y_lo: 2; y = y_hi * 2 + y_lo), z: 8, core: 2. Of those that a mesh axis runs over, the one named last changes fastest.
Arguments:
- state: float32 [8, 16, 384, 2048], P(None, None, 'gy', 'gx'), may hold values from -6 to 6
- register: float32 [8, 16, 384, 2048], P(None, None, 'gy', 'gx'), may hold values from -6 to 6
- checkpoint: bfloat16 [8, 16, 384, 2048], P(None, None, 'gy', 'gx'), may hold values from -6 to 6
- velocity: float32 [3, 16, 384, 2048], P(None, None, 'gy', 'gx'), may hold values from -4 to 4
- diffusivity: float32 [16, 384, 2048], P(None, 'gy', 'gx'), may hold values from 0.02 to 0.3
Outputs:
- new_state: float32 [8, 16, 384, 2048], P(None, None, 'gy', 'gx')
- new_register: float32 [8, 16, 384, 2048], P(None, None, 'gy', 'gx')
- gram: float32 [2048, 2048], P('gx', 'gy')
The draws below stay inside these ranges and needn't reach their ends.
All inputs are finite; a program needn't handle non-finite values.
Results may differ from the reference program's by a relative error of at most 0.0003.
Values sent between devices are 32-bit elements; how exact they have to be, the bound alone decides.
No kernel may reach another device: no remote copies, remote signals or barrier semaphores. Data moves between devices by JAX's collectives and lax.ppermute only.
A program may use at most 64 MiB of HBM per device.

```python
import math
import jax
import jax.numpy as jnp
from jax import lax

NX = 2048
NV = 8
NZ = 16
NY = 384


def shard_levels(stream_key, dims, cuts, smallest, high):
    factor_of, own = 1.0, jax.random.fold_in(stream_key, 6)
    for dim, shards_of in cuts:
        steps = jnp.exp(jax.random.uniform(jax.random.fold_in(own, dim), (shards_of,), jnp.float32, smallest / len(cuts), high / len(cuts)))
        factor_of = factor_of * jnp.repeat(steps, dims[dim] // shards_of).reshape([-1 if axis == dim else 1 for axis in range(len(dims))])
    return factor_of


def centred(rng, dims, scale, most, shards=(), held_as=jnp.bfloat16):
    entries = jax.random.normal(rng, dims, jnp.float32) * scale
    if len(shards) > 0:
        entries = shard_levels(rng, dims, shards, -0.22, 0.18) * entries
    return jnp.clip(entries, min=-most, max=most).astype(held_as)


def setup_inputs(seed: int = 0) -> dict:
    seeds = jax.random.split(jax.random.key(seed), 6)
    state = centred(seeds[0], (NV, NZ, NY, NX), 1.0, 6.0, ((2, 32), (3, 16)), jnp.float32)
    register = centred(seeds[1], (NV, NZ, NY, NX), 1.0, 6.0, ((2, 32), (3, 16)), jnp.float32)
    checkpoint = centred(seeds[2], (NV, NZ, NY, NX), 1.0, 6.0, ((2, 32), (3, 16)))
    velocity = centred(seeds[3], (3, NZ, NY, NX), 1.0, 4.0, ((2, 32), (3, 16)), jnp.float32)
    diffusivity = jnp.clip(jnp.exp(math.log(0.3) - 2.7080503 * jax.random.uniform(seeds[4], (NZ, NY, NX), jnp.float32) ** shard_levels(seeds[4], (NZ, NY, NX), ((1, 32), (2, 16)), -0.2, 0.2)), 0.02, 0.3)
    return {"state": state, "register": register, "checkpoint": checkpoint, "velocity": velocity, "diffusivity": diffusivity}


step_size = 0.3
carry_weight = -5.0 / 9.0
update_weight = 15.0 / 16.0


def first_diff(field, axis):
    plus_one = jnp.roll(field, -1, axis)
    minus_one = jnp.roll(field, 1, axis)
    plus_two = jnp.roll(field, -2, axis)
    minus_two = jnp.roll(field, 2, axis)
    return (8.0 * (plus_one - minus_one) - (plus_two - minus_two)) / 12.0


def second_diff(field, axis):
    plus_one = jnp.roll(field, -1, axis)
    minus_one = jnp.roll(field, 1, axis)
    plus_two = jnp.roll(field, -2, axis)
    minus_two = jnp.roll(field, 2, axis)
    return (16.0 * (plus_one + minus_one) - (plus_two + minus_two) - 30.0 * field) / 12.0


def reference(state, register, checkpoint, velocity, diffusivity):
    advect = velocity[0][None] * first_diff(state, 3) + velocity[1][None] * first_diff(state, 2) + velocity[2][None] * first_diff(state, 1)
    spread = second_diff(state, 3) + second_diff(state, 2) + second_diff(state, 1)
    tendency = -advect + diffusivity[None] * spread
    new_register = carry_weight * register + step_size * tendency
    new_state = state + update_weight * new_register
    change = new_state - checkpoint.astype(jnp.float32)
    columns = NV * NZ * NY
    unfolded = jnp.moveaxis(change, 3, 0).reshape(NX, columns)
    gram = jnp.dot(unfolded, unfolded.T, preferred_element_type=jnp.float32, precision=lax.Precision.HIGHEST)
    gram = gram / jnp.float32(columns)
    return new_state, new_register, gram
```

```python
import jax
import jax.numpy as jnp
from jax import lax
from jax.experimental import pallas as pl
from jax.experimental.pallas import tpu as pltpu
from jax.sharding import PartitionSpec as P

step_size = 0.3
carry_weight = -5.0 / 9.0
update_weight = 15.0 / 16.0

NX_CHIPS, NY_LO, CORES = 4, 2, 2
HIGHEST = lax.Precision.HIGHEST


def gx_of(x, y, core):
    return (x % NX_CHIPS) * NY_LO * CORES + (y % NY_LO) * CORES + core % CORES


def from_offset(dx, dy, dcore):
    return [
        (gx_of(x + dx, y + dy, core + dcore), gx_of(x, y, core))
        for x in range(NX_CHIPS)
        for y in range(NY_LO)
        for core in range(CORES)
    ]


def fetch(value, dx, dy, dcore):
    return lax.ppermute(value, "gx", from_offset(dx, dy, dcore))


def edge_lanes():
    row = lax.broadcasted_iota(jnp.int32, (8, 128), 0)
    lane = lax.broadcasted_iota(jnp.int32, (8, 128), 1)
    wanted = jnp.where(row < 2, row, row + 124)
    return jnp.where((row < 4) & (lane == wanted), 1.0, 0.0).astype(jnp.float32)


def pack_kernel(s_ref, ylo_ref, yhi_ref, xlo_ref, xhi_ref):
    ny = s_ref.shape[1]
    ylo_ref[...] = s_ref[:, 0:2]
    yhi_ref[...] = s_ref[:, ny - 2 : ny]
    flat = s_ref[...].reshape(-1, 128)
    edges = lax.dot_general(
        edge_lanes(), flat, (((1,), (1,)), ((), ())), preferred_element_type=jnp.float32, precision=HIGHEST
    )
    xlo_ref[...] = edges[0:2]
    xhi_ref[...] = edges[2:4]


def pack(s):
    nv, ny, nz, nx = s.shape
    f32 = jnp.float32
    return pl.pallas_call(
        pack_kernel,
        out_shape=(
            jax.ShapeDtypeStruct((nv, 2, nz, nx), f32),
            jax.ShapeDtypeStruct((nv, 2, nz, nx), f32),
            jax.ShapeDtypeStruct((2, nv * ny * nz), f32),
            jax.ShapeDtypeStruct((2, nv * ny * nz), f32),
        ),
        name="pack_edges",
    )(s)


def stencil_kernel(
    s_ref, r_ref, c_ref, vel_ref, dif_ref, ybelow_ref, yabove_ref, xleft_ref, xright_ref,
    ns_ref, nr_ref, chg_ref, halo_ref, edge_ref,
):
    nvb, ny, nz, nx = s_ref.shape
    halo_ref[...] = jnp.zeros_like(halo_ref)
    halo_ref[0:2, :] = xright_ref[...]
    halo_ref[2:4, :] = xleft_ref[...]
    edge_ref[...] = lax.dot_general(
        halo_ref[...], edge_lanes(), (((0,), (0,)), ((), ())), preferred_element_type=jnp.float32, precision=HIGHEST
    )
    lane = lax.broadcasted_iota(jnp.int32, (nz, nx), 1)

    def row(v, y):
        if y < 0:
            return ybelow_ref[v, y + 2]
        if y >= ny:
            return yabove_ref[v, y - ny]
        return s_ref[v, y]

    for v in range(nvb):
        for y in range(ny):
            f = row(v, y)
            e = edge_ref[pl.ds((v * ny + y) * nz, nz), :]
            xp1 = pltpu.roll(jnp.where(lane < 1, e, f), nx - 1, 1)
            xp2 = pltpu.roll(jnp.where(lane < 2, e, f), nx - 2, 1)
            xm1 = pltpu.roll(jnp.where(lane >= nx - 1, e, f), 1, 1)
            xm2 = pltpu.roll(jnp.where(lane >= nx - 2, e, f), 2, 1)
            yp1, yp2, ym1, ym2 = row(v, y + 1), row(v, y + 2), row(v, y - 1), row(v, y - 2)
            zp1 = pltpu.roll(f, nz - 1, 0)
            zp2 = pltpu.roll(f, nz - 2, 0)
            zm1 = pltpu.roll(f, 1, 0)
            zm2 = pltpu.roll(f, 2, 0)
            first_x = 8.0 * (xp1 - xm1) - (xp2 - xm2)
            first_y = 8.0 * (yp1 - ym1) - (yp2 - ym2)
            first_z = 8.0 * (zp1 - zm1) - (zp2 - zm2)
            near = (xp1 + xm1) + (yp1 + ym1) + (zp1 + zm1)
            far = (xp2 + xm2) + (yp2 + ym2) + (zp2 + zm2)
            spread = 16.0 * near - far - 90.0 * f
            advect = vel_ref[0, y] * first_x + vel_ref[1, y] * first_y + vel_ref[2, y] * first_z
            tendency = dif_ref[y] * spread - advect
            new_register = carry_weight * r_ref[v, y] + (step_size / 12.0) * tendency
            new_state = f + update_weight * new_register
            ns_ref[v, y] = new_state
            nr_ref[v, y] = new_register
            chg_ref[v, y] = new_state - c_ref[v, y].astype(jnp.float32)


def stencil(s, r, c, vel, dif, ybelow, yabove, xleft, xright, per_step=2):
    nv, ny, nz, nx = s.shape
    whole = pl.BlockSpec((per_step, ny, nz, nx), lambda i: (i, 0, 0, 0))
    side = pl.BlockSpec((per_step, 2, nz, nx), lambda i: (i, 0, 0, 0))
    cols = per_step * ny * nz
    edge = pl.BlockSpec((2, cols), lambda i: (0, i))
    out = jax.ShapeDtypeStruct(s.shape, jnp.float32)
    return pl.pallas_call(
        stencil_kernel,
        grid=(nv // per_step,),
        in_specs=[
            whole, whole, whole,
            pl.BlockSpec(vel.shape, lambda i: (0, 0, 0, 0)),
            pl.BlockSpec(dif.shape, lambda i: (0, 0, 0)),
            side, side, edge, edge,
        ],
        out_specs=[whole, whole, whole],
        out_shape=[out, out, out],
        scratch_shapes=[pltpu.VMEM((8, cols), jnp.float32), pltpu.VMEM((cols, nx), jnp.float32)],
        name="stencil",
    )(s, r, c, vel, dif, ybelow, yabove, xleft, xright)


def place_kernel(where_ref, own_ref, other_ref, out_ref):
    x, y, core = where_ref[0], where_ref[1], where_ref[2]
    for dx in range(NX_CHIPS):
        for dcore in range(CORES):
            for dy, source in ((0, own_ref), (1, other_ref)):
                at = (
                    ((x + dx) % NX_CHIPS) * NY_LO * CORES
                    + ((y + dy) % NY_LO) * CORES
                    + (core + dcore) % CORES
                )
                out_ref[at] = source[dx, dcore]


def place(where, own, other):
    n = own.shape[0] * own.shape[1] * NY_LO
    vmem = pl.BlockSpec(memory_space=pltpu.VMEM)
    return pl.pallas_call(
        place_kernel,
        in_specs=[pl.BlockSpec(memory_space=pltpu.SMEM), vmem, vmem],
        out_specs=vmem,
        out_shape=jax.ShapeDtypeStruct((n,) + own.shape[2:], jnp.float32),
        name="place",
    )(where, own, other)


def against(columns, rows):
    return lax.dot_general(
        columns, rows, (((0,), (0,)), ((), ())), preferred_element_type=jnp.float32, precision=lax.Precision.HIGH
    )


def on_device(state, register, checkpoint, velocity, diffusivity):
    nv, nz, ny, nx = state.shape
    to_yzx = lambda a: jnp.swapaxes(a, -3, -2)
    s, r, c = to_yzx(state), to_yzx(register), to_yzx(checkpoint)
    ylo, yhi, xlo, xhi = pack(s)
    up = lambda n: [(i, (i + 1) % n) for i in range(n)]
    down = lambda n: [(b, a) for a, b in up(n)]
    n_gx, n_gy = lax.axis_size("gx"), lax.axis_size("gy")
    xleft = lax.ppermute(xhi, "gx", up(n_gx))
    xright = lax.ppermute(xlo, "gx", down(n_gx))
    ybelow = lax.ppermute(yhi, "gy", up(n_gy))
    yabove = lax.ppermute(ylo, "gy", down(n_gy))
    new_state, new_register, change = stencil(
        s, r, c, to_yzx(velocity), to_yzx(diffusivity), ybelow, yabove, xleft, xright
    )
    depth = nv * ny * nz
    half = depth // 2
    mine = change.reshape(depth, nx)
    right = fetch(mine, 1, 0, 0)
    left = fetch(mine, -1, 0, 0)
    across = fetch(mine, 0, 1, 0)
    mine_too = fetch(mine, 0, 0, 1)
    far0 = fetch(right[:half], 1, 0, 0)
    far1 = fetch(left[half:], -1, 0, 0)
    right_too = fetch(right, 0, 0, 1)
    left_too = fetch(left, 0, 0, 1)
    far0_too = fetch(far0, 0, 0, 1)
    far1_too = fetch(far1, 0, 0, 1)
    rows = jnp.concatenate([mine, across], axis=1)
    near = [against(a, rows) for a in (mine, mine_too, right, right_too, left, left_too)]
    far = [
        against(a, rows[:half]) + against(b, rows[half:]) for a, b in ((far0, far1), (far0_too, far1_too))
    ]
    blocks = jnp.stack(near[:4] + far + near[4:]).reshape(NX_CHIPS, CORES, nx, 2 * nx)
    own, theirs = blocks[..., :nx], blocks[..., nx:]
    other = fetch(theirs, 0, 1, 0)
    gx = lax.axis_index("gx")
    where = jnp.stack([gx // (NY_LO * CORES), (gx // CORES) % NY_LO, gx % CORES]).astype(jnp.int32)
    partial = place(where, own, other).reshape(n_gy, -1, nx)
    pieces = lax.all_to_all(partial, "gy", 0, 0, tiled=True)
    columns = nv * nz * ny * n_gy
    gram = jnp.sum(pieces, axis=0) / jnp.float32(columns)
    return to_yzx(new_state), to_yzx(new_register), gram.T


def solution(mesh):
    in_specs = (
        P(None, None, "gy", "gx"),
        P(None, None, "gy", "gx"),
        P(None, None, "gy", "gx"),
        P(None, None, "gy", "gx"),
        P(None, "gy", "gx"),
    )
    out_specs = (P(None, None, "gy", "gx"), P(None, None, "gy", "gx"), P("gx", "gy"))
    return jax.shard_map(
        on_device, mesh=mesh, in_specs=in_specs, out_specs=out_specs, check_vma=False
    )
```

```python
import jax
import jax.numpy as jnp
from jax import lax
from jax.experimental import pallas as pl
from jax.experimental.pallas import tpu as pltpu
from jax.sharding import PartitionSpec as P

step_size = 0.3
carry_weight = -5.0 / 9.0
update_weight = 15.0 / 16.0

NX_CHIPS, NY_LO, CORES = 4, 2, 2
HIGHEST = lax.Precision.HIGHEST


def gx_of(x, y, core):
    return (x % NX_CHIPS) * NY_LO * CORES + (y % NY_LO) * CORES + core % CORES


def from_offset(dx, dy, dcore):
    return [
        (gx_of(x + dx, y + dy, core + dcore), gx_of(x, y, core))
        for x in range(NX_CHIPS)
        for y in range(NY_LO)
        for core in range(CORES)
    ]


def fetch(value, dx, dy, dcore):
    return lax.ppermute(value, "gx", from_offset(dx, dy, dcore))


def edge_lanes():
    row = lax.broadcasted_iota(jnp.int32, (8, 128), 0)
    lane = lax.broadcasted_iota(jnp.int32, (8, 128), 1)
    wanted = jnp.where(row < 2, row, row + 124)
    return jnp.where((row < 4) & (lane == wanted), 1.0, 0.0).astype(jnp.float32)


def pack_kernel(s_ref, ylo_ref, yhi_ref, xlo_ref, xhi_ref):
    ny = s_ref.shape[1]
    ylo_ref[...] = s_ref[:, 0:2]
    yhi_ref[...] = s_ref[:, ny - 2 : ny]
    flat = s_ref[...].reshape(-1, 128)
    edges = lax.dot_general(
        edge_lanes(), flat, (((1,), (1,)), ((), ())), preferred_element_type=jnp.float32, precision=HIGHEST
    )
    xlo_ref[...] = edges[0:2]
    xhi_ref[...] = edges[2:4]


def pack(s):
    nv, ny, nz, nx = s.shape
    f32 = jnp.float32
    return pl.pallas_call(
        pack_kernel,
        out_shape=(
            jax.ShapeDtypeStruct((nv, 2, nz, nx), f32),
            jax.ShapeDtypeStruct((nv, 2, nz, nx), f32),
            jax.ShapeDtypeStruct((2, nv * ny * nz), f32),
            jax.ShapeDtypeStruct((2, nv * ny * nz), f32),
        ),
        name="pack_edges",
    )(s)


def stencil_kernel(
    s_ref, r_ref, c_ref, vel_ref, dif_ref, ybelow_ref, yabove_ref, xleft_ref, xright_ref,
    ns_ref, nr_ref, chg_ref, halo_ref, edge_ref,
):
    nvb, ny, nz, nx = s_ref.shape
    halo_ref[...] = jnp.zeros_like(halo_ref)
    halo_ref[0:2, :] = xright_ref[...]
    halo_ref[2:4, :] = xleft_ref[...]
    edge_ref[...] = lax.dot_general(
        halo_ref[...], edge_lanes(), (((0,), (0,)), ((), ())), preferred_element_type=jnp.float32, precision=HIGHEST
    )
    lane = lax.broadcasted_iota(jnp.int32, (nz, nx), 1)

    def row(v, y):
        if y < 0:
            return ybelow_ref[v, y + 2]
        if y >= ny:
            return yabove_ref[v, y - ny]
        return s_ref[v, y]

    for v in range(nvb):
        for y in range(ny):
            f = row(v, y)
            e = edge_ref[pl.ds((v * ny + y) * nz, nz), :]
            xp1 = pltpu.roll(jnp.where(lane < 1, e, f), nx - 1, 1)
            xp2 = pltpu.roll(jnp.where(lane < 2, e, f), nx - 2, 1)
            xm1 = pltpu.roll(jnp.where(lane >= nx - 1, e, f), 1, 1)
            xm2 = pltpu.roll(jnp.where(lane >= nx - 2, e, f), 2, 1)
            yp1, yp2, ym1, ym2 = row(v, y + 1), row(v, y + 2), row(v, y - 1), row(v, y - 2)
            zp1 = pltpu.roll(f, nz - 1, 0)
            zp2 = pltpu.roll(f, nz - 2, 0)
            zm1 = pltpu.roll(f, 1, 0)
            zm2 = pltpu.roll(f, 2, 0)
            first_x = 8.0 * (xp1 - xm1) - (xp2 - xm2)
            first_y = 8.0 * (yp1 - ym1) - (yp2 - ym2)
            first_z = 8.0 * (zp1 - zm1) - (zp2 - zm2)
            near = (xp1 + xm1) + (yp1 + ym1) + (zp1 + zm1)
            far = (xp2 + xm2) + (yp2 + ym2) + (zp2 + zm2)
            spread = 16.0 * near - far - 90.0 * f
            advect = vel_ref[0, y] * first_x + vel_ref[1, y] * first_y + vel_ref[2, y] * first_z
            tendency = dif_ref[y] * spread - advect
            new_register = carry_weight * r_ref[v, y] + (step_size / 12.0) * tendency
            new_state = f + update_weight * new_register
            ns_ref[v, y] = new_state
            nr_ref[v, y] = new_register
            chg_ref[v, y] = new_state - c_ref[v, y].astype(jnp.float32)


def stencil(s, r, c, vel, dif, ybelow, yabove, xleft, xright, per_step=2):
    nv, ny, nz, nx = s.shape
    whole = pl.BlockSpec((per_step, ny, nz, nx), lambda i: (i, 0, 0, 0))
    side = pl.BlockSpec((per_step, 2, nz, nx), lambda i: (i, 0, 0, 0))
    cols = per_step * ny * nz
    edge = pl.BlockSpec((2, cols), lambda i: (0, i))
    out = jax.ShapeDtypeStruct(s.shape, jnp.float32)
    return pl.pallas_call(
        stencil_kernel,
        grid=(nv // per_step,),
        in_specs=[
            whole, whole, whole,
            pl.BlockSpec(vel.shape, lambda i: (0, 0, 0, 0)),
            pl.BlockSpec(dif.shape, lambda i: (0, 0, 0)),
            side, side, edge, edge,
        ],
        out_specs=[whole, whole, whole],
        out_shape=[out, out, out],
        scratch_shapes=[pltpu.VMEM((8, cols), jnp.float32), pltpu.VMEM((cols, nx), jnp.float32)],
        name="stencil",
    )(s, r, c, vel, dif, ybelow, yabove, xleft, xright)


def place_kernel(near_ref, far_ref, near_y_ref, far_y_ref, near_c_ref, far_c_ref, near_yc_ref, far_yc_ref, out_ref):
    gx = lax.axis_index("gx")
    core = lax.rem(gx, CORES)
    y = lax.rem(lax.div(gx, CORES), NY_LO)
    x = lax.div(gx, CORES * NY_LO)
    nx = out_ref.shape[-1]
    sources = (
        (0, 0, near_ref, far_ref),
        (1, 0, near_y_ref, far_y_ref),
        (0, 1, near_c_ref, far_c_ref),
        (1, 1, near_yc_ref, far_yc_ref),
    )
    for dy, dcore, near, far in sources:
        lanes = slice(dcore * nx, dcore * nx + nx)
        for dx in range(NX_CHIPS):
            at = (
                lax.rem(x + dx, NX_CHIPS) * (NY_LO * CORES)
                + lax.rem(y + dy, NY_LO) * CORES
                + lax.rem(core + dcore, CORES)
            )
            out_ref[at] = far[:, lanes] if dx == 2 else near[NEAR.index(dx), :, lanes]


NEAR = (0, 1, 3)


def place(*parts):
    nx = parts[0].shape[-2]
    vmem = pl.BlockSpec(memory_space=pltpu.VMEM)
    return pl.pallas_call(
        place_kernel,
        in_specs=[vmem] * len(parts),
        out_specs=vmem,
        out_shape=jax.ShapeDtypeStruct((NX_CHIPS * NY_LO * CORES, nx, nx), jnp.float32),
        name="place",
    )(*parts)


def against(columns, rows):
    return lax.dot_general(
        columns, rows, (((0,), (0,)), ((), ())), preferred_element_type=jnp.float32, precision=lax.Precision.HIGH
    )


def on_device(state, register, checkpoint, velocity, diffusivity):
    nv, nz, ny, nx = state.shape
    to_yzx = lambda a: jnp.swapaxes(a, -3, -2)
    s, r, c = to_yzx(state), to_yzx(register), to_yzx(checkpoint)
    ylo, yhi, xlo, xhi = pack(s)
    up = lambda n: [(i, (i + 1) % n) for i in range(n)]
    down = lambda n: [(b, a) for a, b in up(n)]
    n_gx, n_gy = lax.axis_size("gx"), lax.axis_size("gy")
    xleft = lax.ppermute(xhi, "gx", up(n_gx))
    xright = lax.ppermute(xlo, "gx", down(n_gx))
    ybelow = lax.ppermute(yhi, "gy", up(n_gy))
    yabove = lax.ppermute(ylo, "gy", down(n_gy))
    new_state, new_register, change = stencil(
        s, r, c, to_yzx(velocity), to_yzx(diffusivity), ybelow, yabove, xleft, xright
    )
    depth = nv * ny * nz
    half = depth // 2
    mine = change.reshape(depth, nx)
    front, back = mine[:half], mine[half:]
    right0 = fetch(front, 1, 0, 0)
    left1 = fetch(back, -1, 0, 0)
    across = fetch(mine, 0, 1, 0)
    mine_c = fetch(mine, 0, 0, 1)
    right1 = fetch(back, 1, 0, 0)
    left0 = fetch(front, -1, 0, 0)
    far0 = fetch(right0, 1, 0, 0)
    far1 = fetch(left1, -1, 0, 0)
    across_c = fetch(across, 0, 0, 1)

    def by_halves(a, b, rows):
        return against(a, rows[:half]) + against(b, rows[half:])

    def products(rows):
        near = jnp.stack([against(mine, rows), by_halves(right0, right1, rows), by_halves(left0, left1, rows)])
        return near, by_halves(far0, far1, rows)

    near, far = products(jnp.concatenate([mine, mine_c], axis=1))
    near_y, far_y = products(jnp.concatenate([across, across_c], axis=1))
    near_c, far_c = fetch(near, 0, 0, 1), fetch(far, 0, 0, 1)
    near_y, far_y = fetch(near_y, 0, 1, 0), fetch(far_y, 0, 1, 0)
    near_yc, far_yc = fetch(near_y, 0, 0, 1), fetch(far_y, 0, 0, 1)
    partial = place(near, far, near_y, far_y, near_c, far_c, near_yc, far_yc).reshape(n_gy, -1, nx)
    pieces = lax.all_to_all(partial, "gy", 0, 0, tiled=True)
    columns = nv * nz * ny * n_gy
    gram = jnp.sum(pieces, axis=0) / jnp.float32(columns)
    return to_yzx(new_state), to_yzx(new_register), gram.T


def solution(mesh):
    in_specs = (
        P(None, None, "gy", "gx"),
        P(None, None, "gy", "gx"),
        P(None, None, "gy", "gx"),
        P(None, None, "gy", "gx"),
        P(None, "gy", "gx"),
    )
    out_specs = (P(None, None, "gy", "gx"), P(None, None, "gy", "gx"), P("gx", "gy"))
    return jax.shard_map(
        on_device, mesh=mesh, in_specs=in_specs, out_specs=out_specs, check_vma=False
    )
```

```python
import jax
import jax.numpy as jnp
from jax import lax
from jax.experimental import pallas as pl
from jax.experimental.pallas import tpu as pltpu
from jax.sharding import PartitionSpec as P


step_size = 0.3
carry_weight = -5.0 / 9.0
update_weight = 15.0 / 16.0

NX_CHIPS, NY_LO, CORES = 4, 2, 2
HIGHEST = lax.Precision.HIGHEST


def gx_of(x, y, core):
    return (x % NX_CHIPS) * NY_LO * CORES + (y % NY_LO) * CORES + core % CORES


def from_offset(dx, dy, dcore):
    return [
        (gx_of(x + dx, y + dy, core + dcore), gx_of(x, y, core))
        for x in range(NX_CHIPS)
        for y in range(NY_LO)
        for core in range(CORES)
    ]


def fetch(value, dx, dy, dcore):
    return lax.ppermute(value, "gx", from_offset(dx, dy, dcore))


def edge_lanes():
    row = lax.broadcasted_iota(jnp.int32, (8, 128), 0)
    lane = lax.broadcasted_iota(jnp.int32, (8, 128), 1)
    wanted = jnp.where(row < 2, row, row + 124)
    return jnp.where((row < 4) & (lane == wanted), 1.0, 0.0).astype(jnp.float32)


def pack_kernel(s_ref, ylo_ref, yhi_ref, xlo_ref, xhi_ref):
    ny = s_ref.shape[1]
    ylo_ref[...] = s_ref[:, 0:2]
    yhi_ref[...] = s_ref[:, ny - 2 : ny]
    flat = s_ref[...].reshape(-1, 128)
    edges = lax.dot_general(
        edge_lanes(), flat, (((1,), (1,)), ((), ())), preferred_element_type=jnp.float32, precision=HIGHEST
    )
    xlo_ref[...] = edges[0:2]
    xhi_ref[...] = edges[2:4]


def pack(s):
    nv, ny, nz, nx = s.shape
    f32 = jnp.float32
    return pl.pallas_call(
        pack_kernel,
        out_shape=(
            jax.ShapeDtypeStruct((nv, 2, nz, nx), f32),
            jax.ShapeDtypeStruct((nv, 2, nz, nx), f32),
            jax.ShapeDtypeStruct((2, nv * ny * nz), f32),
            jax.ShapeDtypeStruct((2, nv * ny * nz), f32),
        ),
        name="pack_edges",
    )(s)


def stencil_kernel(
    s_ref, r_ref, c_ref, vel_ref, dif_ref, ybelow_ref, yabove_ref, xleft_ref, xright_ref,
    ns_ref, nr_ref, chg_ref, halo_ref, edge_ref,
):
    nvb, ny, nz, nx = s_ref.shape
    halo_ref[...] = jnp.zeros_like(halo_ref)
    halo_ref[0:2, :] = xright_ref[...]
    halo_ref[2:4, :] = xleft_ref[...]
    edge_ref[...] = lax.dot_general(
        halo_ref[...], edge_lanes(), (((0,), (0,)), ((), ())), preferred_element_type=jnp.float32, precision=HIGHEST
    )
    lane = lax.broadcasted_iota(jnp.int32, (nz, nx), 1)

    def row(v, y):
        if y < 0:
            return ybelow_ref[v, y + 2]
        if y >= ny:
            return yabove_ref[v, y - ny]
        return s_ref[v, y]

    for v in range(nvb):
        for y in range(ny):
            f = row(v, y)
            e = edge_ref[pl.ds((v * ny + y) * nz, nz), :]
            xp1 = pltpu.roll(jnp.where(lane < 1, e, f), nx - 1, 1)
            xp2 = pltpu.roll(jnp.where(lane < 2, e, f), nx - 2, 1)
            xm1 = pltpu.roll(jnp.where(lane >= nx - 1, e, f), 1, 1)
            xm2 = pltpu.roll(jnp.where(lane >= nx - 2, e, f), 2, 1)
            yp1, yp2, ym1, ym2 = row(v, y + 1), row(v, y + 2), row(v, y - 1), row(v, y - 2)
            zp1 = pltpu.roll(f, nz - 1, 0)
            zp2 = pltpu.roll(f, nz - 2, 0)
            zm1 = pltpu.roll(f, 1, 0)
            zm2 = pltpu.roll(f, 2, 0)
            first_x = 8.0 * (xp1 - xm1) - (xp2 - xm2)
            first_y = 8.0 * (yp1 - ym1) - (yp2 - ym2)
            first_z = 8.0 * (zp1 - zm1) - (zp2 - zm2)
            near = (xp1 + xm1) + (yp1 + ym1) + (zp1 + zm1)
            far = (xp2 + xm2) + (yp2 + ym2) + (zp2 + zm2)
            spread = 16.0 * near - far - 90.0 * f
            advect = vel_ref[0, y] * first_x + vel_ref[1, y] * first_y + vel_ref[2, y] * first_z
            tendency = dif_ref[y] * spread - advect
            new_register = carry_weight * r_ref[v, y] + (step_size / 12.0) * tendency
            new_state = f + update_weight * new_register
            ns_ref[v, y] = new_state
            nr_ref[v, y] = new_register
            chg_ref[v, y] = new_state - c_ref[v, y].astype(jnp.float32)


def stencil(s, r, c, vel, dif, ybelow, yabove, xleft, xright, per_step=4):
    nv, ny, nz, nx = s.shape
    whole = pl.BlockSpec((per_step, ny, nz, nx), lambda i: (i, 0, 0, 0))
    side = pl.BlockSpec((per_step, 2, nz, nx), lambda i: (i, 0, 0, 0))
    cols = per_step * ny * nz
    edge = pl.BlockSpec((2, cols), lambda i: (0, i))
    out = jax.ShapeDtypeStruct(s.shape, jnp.float32)
    return pl.pallas_call(
        stencil_kernel,
        grid=(nv // per_step,),
        in_specs=[
            whole, whole, whole,
            pl.BlockSpec(vel.shape, lambda i: (0, 0, 0, 0)),
            pl.BlockSpec(dif.shape, lambda i: (0, 0, 0)),
            side, side, edge, edge,
        ],
        out_specs=[whole, whole, whole],
        out_shape=[out, out, out],
        scratch_shapes=[pltpu.VMEM((8, cols), jnp.float32), pltpu.VMEM((cols, nx), jnp.float32)],
        name="stencil",
    )(s, r, c, vel, dif, ybelow, yabove, xleft, xright)


def place_kernel(*refs):
    *parts, out_ref = refs
    gx = lax.axis_index("gx")
    core = lax.rem(gx, CORES)
    y = lax.rem(lax.div(gx, CORES), NY_LO)
    x = lax.div(gx, CORES * NY_LO)
    for n, (dx, dcore) in enumerate(ORDER):
        part, at = next((p, n - first) for p, first in zip(parts[::2], PARTS) if first <= n < first + p.shape[0])
        other = parts[1::2][[p is part for p in parts[::2]].index(True)]
        for dy, value in ((0, part[at]), (1, other[at])):
            place_at = (
                lax.rem(x + dx, NX_CHIPS) * (NY_LO * CORES)
                + lax.rem(y + dy, NY_LO) * CORES
                + lax.rem(core + dcore, CORES)
            )
            out_ref[place_at] = value


ORDER = ((0, 0), (0, 1), (1, 0), (3, 0), (1, 1), (3, 1), (2, 0), (2, 1))
PARTS = (0, 4)


def place(*parts):
    nx = parts[0].shape[-2]
    vmem = pl.BlockSpec(memory_space=pltpu.VMEM)
    return pl.pallas_call(
        place_kernel,
        in_specs=[vmem] * len(parts),
        out_specs=vmem,
        out_shape=jax.ShapeDtypeStruct((NX_CHIPS * NY_LO * CORES, nx, nx), jnp.float32),
        name="place",
    )(*parts)


def against(columns, rows):
    return lax.dot_general(
        columns, rows, (((0,), (0,)), ((), ())), preferred_element_type=jnp.float32, precision=lax.Precision.HIGH
    )


def section(state, register, checkpoint, velocity, diffusivity):
    nv, nz, ny, nx = state.shape
    to_yzx = lambda a: jnp.swapaxes(a, -3, -2)
    s, r, c = to_yzx(state), to_yzx(register), to_yzx(checkpoint)
    ylo, yhi, xlo, xhi = pack(s)
    up = lambda n: [(i, (i + 1) % n) for i in range(n)]
    down = lambda n: [(b, a) for a, b in up(n)]
    n_gx, n_gy = lax.axis_size("gx"), lax.axis_size("gy")
    xleft = lax.ppermute(xhi, "gx", up(n_gx))
    xright = lax.ppermute(xlo, "gx", down(n_gx))
    ybelow = lax.ppermute(yhi, "gy", up(n_gy))
    yabove = lax.ppermute(ylo, "gy", down(n_gy))
    new_state, new_register, change = stencil(
        s, r, c, to_yzx(velocity), to_yzx(diffusivity), ybelow, yabove, xleft, xright
    )
    depth = nv * ny * nz
    half = depth // 2
    mine = change.reshape(depth, nx)
    right = fetch(mine, 1, 0, 0)
    left = fetch(mine, -1, 0, 0)
    across = fetch(mine, 0, 1, 0)
    mine_c = fetch(mine, 0, 0, 1)
    far0 = fetch(right[:half], 1, 0, 0)
    far1 = fetch(left[half:], -1, 0, 0)
    right_c = fetch(right, 0, 0, 1)
    left_c = fetch(left, 0, 0, 1)
    far0_c = fetch(far0, 0, 0, 1)
    far1_c = fetch(far1, 0, 0, 1)

    def split(a, b, rows):
        return against(a, rows[:half]) + against(b, rows[half:])

    def first(rows):
        return jnp.stack([against(a, rows) for a in (mine, mine_c, right, left)])

    def second(rows):
        wide = [against(a, rows) for a in (right_c, left_c)]
        return jnp.stack(wide + [split(far0, far1, rows), split(far0_c, far1_c, rows)])

    first_y = fetch(first(across), 0, 1, 0)
    second_y = fetch(second(across), 0, 1, 0)
    partial = place(first(mine), first_y, second(mine), second_y).reshape(n_gy, -1, nx)
    pieces = lax.all_to_all(partial, "gy", 0, 0, tiled=True)
    columns = nv * nz * ny * n_gy
    gram = jnp.sum(pieces, axis=0) / jnp.float32(columns)
    return to_yzx(new_state), to_yzx(new_register), gram.T


def solution(mesh):
    in_specs = (
        P(None, None, "gy", "gx"),
        P(None, None, "gy", "gx"),
        P(None, None, "gy", "gx"),
        P(None, None, "gy", "gx"),
        P(None, "gy", "gx"),
    )
    out_specs = (P(None, None, "gy", "gx"), P(None, None, "gy", "gx"), P("gx", "gy"))
    return jax.shard_map(section, mesh=mesh, in_specs=in_specs, out_specs=out_specs, check_vma=False)
```

```python
import jax
import jax.numpy as jnp
from jax import lax
from jax.experimental import pallas as pl
from jax.experimental.pallas import tpu as pltpu
from jax.sharding import PartitionSpec as P


step_size = 0.3
carry_weight = -5.0 / 9.0
update_weight = 15.0 / 16.0

NX_CHIPS, NY_LO, CORES = 4, 2, 2
HIGHEST = lax.Precision.HIGHEST


def gx_of(x, y, core):
    return (x % NX_CHIPS) * NY_LO * CORES + (y % NY_LO) * CORES + core % CORES


def from_offset(dx, dy, dcore):
    return [
        (gx_of(x + dx, y + dy, core + dcore), gx_of(x, y, core))
        for x in range(NX_CHIPS)
        for y in range(NY_LO)
        for core in range(CORES)
    ]


def fetch(value, dx, dy, dcore):
    return lax.ppermute(value, "gx", from_offset(dx, dy, dcore))


def edge_lanes():
    row = lax.broadcasted_iota(jnp.int32, (8, 128), 0)
    lane = lax.broadcasted_iota(jnp.int32, (8, 128), 1)
    wanted = jnp.where(row < 2, row, row + 124)
    return jnp.where((row < 4) & (lane == wanted), 1.0, 0.0).astype(jnp.float32)


def pack_kernel(s_ref, ylo_ref, yhi_ref, xlo_ref, xhi_ref):
    ny = s_ref.shape[1]
    ylo_ref[...] = s_ref[:, 0:2]
    yhi_ref[...] = s_ref[:, ny - 2 : ny]
    flat = s_ref[...].reshape(-1, 128)
    for start in range(0, flat.shape[0], 128):
        turned = flat[start : start + 128].T
        xlo_ref[:, start : start + 128] = turned[0:2]
        xhi_ref[:, start : start + 128] = turned[126:128]


def pack(s):
    nv, ny, nz, nx = s.shape
    f32 = jnp.float32
    return pl.pallas_call(
        pack_kernel,
        out_shape=(
            jax.ShapeDtypeStruct((nv, 2, nz, nx), f32),
            jax.ShapeDtypeStruct((nv, 2, nz, nx), f32),
            jax.ShapeDtypeStruct((2, nv * ny * nz), f32),
            jax.ShapeDtypeStruct((2, nv * ny * nz), f32),
        ),
        name="pack_edges",
    )(s)


def stencil_kernel(
    s_ref, r_ref, c_ref, vel_ref, dif_ref, ybelow_ref, yabove_ref, xleft_ref, xright_ref,
    ns_ref, nr_ref, chg_ref, halo_ref, edge_ref,
):
    nvb, ny, nz, nx = s_ref.shape
    halo_ref[...] = jnp.zeros_like(halo_ref)
    halo_ref[0:2, :] = xright_ref[...]
    halo_ref[2:4, :] = xleft_ref[...]
    edge_ref[...] = lax.dot_general(
        halo_ref[...], edge_lanes(), (((0,), (0,)), ((), ())), preferred_element_type=jnp.float32, precision=HIGHEST
    )
    lane = lax.broadcasted_iota(jnp.int32, (nz, nx), 1)

    def row(v, y):
        if y < 0:
            return ybelow_ref[v, y + 2]
        if y >= ny:
            return yabove_ref[v, y - ny]
        return s_ref[v, y]

    for v in range(nvb):
        for y in range(ny):
            f = row(v, y)
            e = edge_ref[pl.ds((v * ny + y) * nz, nz), :]
            xp1 = pltpu.roll(jnp.where(lane < 1, e, f), nx - 1, 1)
            xp2 = pltpu.roll(jnp.where(lane < 2, e, f), nx - 2, 1)
            xm1 = pltpu.roll(jnp.where(lane >= nx - 1, e, f), 1, 1)
            xm2 = pltpu.roll(jnp.where(lane >= nx - 2, e, f), 2, 1)
            yp1, yp2, ym1, ym2 = row(v, y + 1), row(v, y + 2), row(v, y - 1), row(v, y - 2)
            zp1 = pltpu.roll(f, nz - 1, 0)
            zp2 = pltpu.roll(f, nz - 2, 0)
            zm1 = pltpu.roll(f, 1, 0)
            zm2 = pltpu.roll(f, 2, 0)
            first_x = 8.0 * (xp1 - xm1) - (xp2 - xm2)
            first_y = 8.0 * (yp1 - ym1) - (yp2 - ym2)
            first_z = 8.0 * (zp1 - zm1) - (zp2 - zm2)
            near = (xp1 + xm1) + (yp1 + ym1) + (zp1 + zm1)
            far = (xp2 + xm2) + (yp2 + ym2) + (zp2 + zm2)
            spread = 16.0 * near - far - 90.0 * f
            advect = vel_ref[0, y] * first_x + vel_ref[1, y] * first_y + vel_ref[2, y] * first_z
            tendency = dif_ref[y] * spread - advect
            new_register = carry_weight * r_ref[v, y] + (step_size / 12.0) * tendency
            new_state = f + update_weight * new_register
            ns_ref[v, y] = new_state
            nr_ref[v, y] = new_register
            chg_ref[v, y] = new_state - c_ref[v, y].astype(jnp.float32)


def stencil(s, r, c, vel, dif, ybelow, yabove, xleft, xright, per_step=4):
    nv, ny, nz, nx = s.shape
    whole = pl.BlockSpec((per_step, ny, nz, nx), lambda i: (i, 0, 0, 0))
    side = pl.BlockSpec((per_step, 2, nz, nx), lambda i: (i, 0, 0, 0))
    cols = per_step * ny * nz
    edge = pl.BlockSpec((2, cols), lambda i: (0, i))
    out = jax.ShapeDtypeStruct(s.shape, jnp.float32)
    return pl.pallas_call(
        stencil_kernel,
        grid=(nv // per_step,),
        in_specs=[
            whole, whole, whole,
            pl.BlockSpec(vel.shape, lambda i: (0, 0, 0, 0)),
            pl.BlockSpec(dif.shape, lambda i: (0, 0, 0)),
            side, side, edge, edge,
        ],
        out_specs=[whole, whole, whole],
        out_shape=[out, out, out],
        scratch_shapes=[pltpu.VMEM((8, cols), jnp.float32), pltpu.VMEM((cols, nx), jnp.float32)],
        name="stencil",
    )(s, r, c, vel, dif, ybelow, yabove, xleft, xright)


def place_kernel(*refs):
    *parts, out_ref = refs
    gx = lax.axis_index("gx")
    core = lax.rem(gx, CORES)
    y = lax.rem(lax.div(gx, CORES), NY_LO)
    x = lax.div(gx, CORES * NY_LO)
    nx = out_ref.shape[-1]
    for n, (dx, dcore) in enumerate(ORDER):
        part, at = next((p, n - first) for p, first in zip(parts[::2], PARTS) if first <= n < first + p.shape[0])
        other = parts[1::2][[p is part for p in parts[::2]].index(True)]
        for dy, value in ((0, part[at, :, :nx]), (1, other[at])):
            place_at = (
                lax.rem(x + dx, NX_CHIPS) * (NY_LO * CORES)
                + lax.rem(y + dy, NY_LO) * CORES
                + lax.rem(core + dcore, CORES)
            )
            out_ref[place_at] = value


ORDER = ((0, 0), (0, 1), (1, 0), (3, 0), (1, 1), (3, 1), (2, 0), (2, 1))
PARTS = (0, 6)


def place(*parts):
    nx = parts[0].shape[-2]
    vmem = pl.BlockSpec(memory_space=pltpu.VMEM)
    return pl.pallas_call(
        place_kernel,
        in_specs=[vmem] * len(parts),
        out_specs=vmem,
        out_shape=jax.ShapeDtypeStruct((NX_CHIPS * NY_LO * CORES, nx, nx), jnp.float32),
        name="place",
    )(*parts)


def against(columns, rows):
    return lax.dot_general(
        columns, rows, (((0,), (0,)), ((), ())), preferred_element_type=jnp.float32, precision=lax.Precision.HIGH
    )


def section(state, register, checkpoint, velocity, diffusivity):
    nv, nz, ny, nx = state.shape
    to_yzx = lambda a: jnp.swapaxes(a, -3, -2)
    s, r, c = to_yzx(state), to_yzx(register), to_yzx(checkpoint)
    ylo, yhi, xlo, xhi = pack(s)
    up = lambda n: [(i, (i + 1) % n) for i in range(n)]
    down = lambda n: [(b, a) for a, b in up(n)]
    n_gx, n_gy = lax.axis_size("gx"), lax.axis_size("gy")
    xleft = lax.ppermute(xhi, "gx", up(n_gx))
    xright = lax.ppermute(xlo, "gx", down(n_gx))
    ybelow = lax.ppermute(yhi, "gy", up(n_gy))
    yabove = lax.ppermute(ylo, "gy", down(n_gy))
    new_state, new_register, change = stencil(
        s, r, c, to_yzx(velocity), to_yzx(diffusivity), ybelow, yabove, xleft, xright
    )
    depth = nv * ny * nz
    half = depth // 2
    mine = change.reshape(depth, nx)
    right = fetch(mine, 1, 0, 0)
    left = fetch(mine, -1, 0, 0)
    across = fetch(mine, 0, 1, 0)
    mine_c = fetch(mine, 0, 0, 1)
    far0 = fetch(right[:half], 1, 0, 0)
    far1 = fetch(left[half:], -1, 0, 0)
    right_c = fetch(right, 0, 0, 1)
    left_c = fetch(left, 0, 0, 1)
    far = jnp.concatenate([far0, far1], axis=0)
    far_c = fetch(far, 0, 0, 1)
    rows = jnp.concatenate([mine, across], axis=1)

    def products(*columns):
        return jnp.stack([against(a, rows) for a in columns])

    first = products(mine, mine_c, right, left, right_c, left_c)
    second = products(far, far_c)
    first_y = fetch(first[:, :, nx:], 0, 1, 0)
    second_y = fetch(second[:, :, nx:], 0, 1, 0)
    partial = place(first, first_y, second, second_y).reshape(n_gy, -1, nx)
    pieces = lax.all_to_all(partial, "gy", 0, 0, tiled=True)
    columns = nv * nz * ny * n_gy
    gram = jnp.sum(pieces, axis=0) / jnp.float32(columns)
    return to_yzx(new_state), to_yzx(new_register), gram.T


def solution(mesh):
    in_specs = (
        P(None, None, "gy", "gx"),
        P(None, None, "gy", "gx"),
        P(None, None, "gy", "gx"),
        P(None, None, "gy", "gx"),
        P(None, "gy", "gx"),
    )
    out_specs = (P(None, None, "gy", "gx"), P(None, None, "gy", "gx"), P("gx", "gy"))
    return jax.shard_map(
        section, mesh=mesh, in_specs=in_specs, out_specs=out_specs, check_vma=False
    )
```

```python
import jax
import jax.numpy as jnp
from jax import lax
from jax.experimental import pallas as pl
from jax.experimental.pallas import tpu as pltpu
from jax.sharding import PartitionSpec as P


step_size = 0.3
carry_weight = -5.0 / 9.0
update_weight = 15.0 / 16.0

NX_CHIPS, NY_LO, CORES = 4, 2, 2
HIGHEST = lax.Precision.HIGHEST
FIRST = ((0, 0), (0, 1), (1, 0), (3, 0), (1, 1), (3, 1))
SECOND = ((2, 0), (2, 1))


def gx_of(x, y, core):
    return (x % NX_CHIPS) * NY_LO * CORES + (y % NY_LO) * CORES + core % CORES


def from_offset(dx, dy, dcore):
    return [
        (gx_of(x + dx, y + dy, core + dcore), gx_of(x, y, core))
        for x in range(NX_CHIPS)
        for y in range(NY_LO)
        for core in range(CORES)
    ]


def fetch(value, dx, dy, dcore):
    return lax.ppermute(value, "gx", from_offset(dx, dy, dcore))


def edge_lanes():
    row = lax.broadcasted_iota(jnp.int32, (8, 128), 0)
    lane = lax.broadcasted_iota(jnp.int32, (8, 128), 1)
    wanted = jnp.where(row < 2, row, row + 124)
    return jnp.where((row < 4) & (lane == wanted), 1.0, 0.0).astype(jnp.float32)


def pack_kernel(s_ref, ylo_ref, yhi_ref, xlo_ref, xhi_ref):
    ny = s_ref.shape[1]
    ylo_ref[...] = s_ref[:, 0:2]
    yhi_ref[...] = s_ref[:, ny - 2 : ny]
    flat = s_ref[...].reshape(-1, 128)
    for start in range(0, flat.shape[0], 128):
        turned = flat[start : start + 128].T
        xlo_ref[:, start : start + 128] = turned[0:2]
        xhi_ref[:, start : start + 128] = turned[126:128]


def pack(s):
    nv, ny, nz, nx = s.shape
    f32 = jnp.float32
    return pl.pallas_call(
        pack_kernel,
        out_shape=(
            jax.ShapeDtypeStruct((nv, 2, nz, nx), f32),
            jax.ShapeDtypeStruct((nv, 2, nz, nx), f32),
            jax.ShapeDtypeStruct((2, nv * ny * nz), f32),
            jax.ShapeDtypeStruct((2, nv * ny * nz), f32),
        ),
        name="pack_edges",
    )(s)


def stencil_kernel(
    s_ref, r_ref, c_ref, vel_ref, dif_ref, ybelow_ref, yabove_ref, xleft_ref, xright_ref,
    ns_ref, nr_ref, chg_ref, halo_ref, edge_ref,
):
    nvb, ny, nz, nx = s_ref.shape
    halo_ref[...] = jnp.zeros_like(halo_ref)
    halo_ref[0:2, :] = xright_ref[...]
    halo_ref[2:4, :] = xleft_ref[...]
    edge_ref[...] = lax.dot_general(
        halo_ref[...], edge_lanes(), (((0,), (0,)), ((), ())), preferred_element_type=jnp.float32, precision=HIGHEST
    )
    lane = lax.broadcasted_iota(jnp.int32, (nz, nx), 1)

    def row(v, y):
        if y < 0:
            return ybelow_ref[v, y + 2]
        if y >= ny:
            return yabove_ref[v, y - ny]
        return s_ref[v, y]

    for v in range(nvb):
        for y in range(ny):
            f = row(v, y)
            e = edge_ref[pl.ds((v * ny + y) * nz, nz), :]
            xp1 = pltpu.roll(jnp.where(lane < 1, e, f), nx - 1, 1)
            xp2 = pltpu.roll(jnp.where(lane < 2, e, f), nx - 2, 1)
            xm1 = pltpu.roll(jnp.where(lane >= nx - 1, e, f), 1, 1)
            xm2 = pltpu.roll(jnp.where(lane >= nx - 2, e, f), 2, 1)
            yp1, yp2, ym1, ym2 = row(v, y + 1), row(v, y + 2), row(v, y - 1), row(v, y - 2)
            zp1 = pltpu.roll(f, nz - 1, 0)
            zp2 = pltpu.roll(f, nz - 2, 0)
            zm1 = pltpu.roll(f, 1, 0)
            zm2 = pltpu.roll(f, 2, 0)
            first_x = 8.0 * (xp1 - xm1) - (xp2 - xm2)
            first_y = 8.0 * (yp1 - ym1) - (yp2 - ym2)
            first_z = 8.0 * (zp1 - zm1) - (zp2 - zm2)
            near = (xp1 + xm1) + (yp1 + ym1) + (zp1 + zm1)
            far = (xp2 + xm2) + (yp2 + ym2) + (zp2 + zm2)
            spread = 16.0 * near - far - 90.0 * f
            advect = vel_ref[0, y] * first_x + vel_ref[1, y] * first_y + vel_ref[2, y] * first_z
            tendency = dif_ref[y] * spread - advect
            new_register = carry_weight * r_ref[v, y] + (step_size / 12.0) * tendency
            new_state = f + update_weight * new_register
            ns_ref[v, y] = new_state
            nr_ref[v, y] = new_register
            chg_ref[v, y] = new_state - c_ref[v, y].astype(jnp.float32)


def stencil(s, r, c, vel, dif, ybelow, yabove, xleft, xright, per_step=4):
    nv, ny, nz, nx = s.shape
    whole = pl.BlockSpec((per_step, ny, nz, nx), lambda i: (i, 0, 0, 0))
    side = pl.BlockSpec((per_step, 2, nz, nx), lambda i: (i, 0, 0, 0))
    cols = per_step * ny * nz
    edge = pl.BlockSpec((2, cols), lambda i: (0, i))
    out = jax.ShapeDtypeStruct(s.shape, jnp.float32)
    return pl.pallas_call(
        stencil_kernel,
        grid=(nv // per_step,),
        in_specs=[
            whole, whole, whole,
            pl.BlockSpec(vel.shape, lambda i: (0, 0, 0, 0)),
            pl.BlockSpec(dif.shape, lambda i: (0, 0, 0)),
            side, side, edge, edge,
        ],
        out_specs=[whole, whole, whole],
        out_shape=[out, out, out],
        scratch_shapes=[pltpu.VMEM((8, cols), jnp.float32), pltpu.VMEM((cols, nx), jnp.float32)],
        name="stencil",
    )(s, r, c, vel, dif, ybelow, yabove, xleft, xright)


ORDER = tuple(
    (dx, dy, dcore)
    for dy, columns in ((0, FIRST), (0, SECOND), (1, FIRST), (1, SECOND))
    for dx, dcore in columns
)


def owners(n_gy):
    groups = []
    for x in range(NX_CHIPS):
        for y in range(NY_LO):
            for core in range(CORES):
                blocks = [gx_of(x + dx, y + dy, core + dcore) for dx, dy, dcore in ORDER]
                mine = gx_of(x, y, core)
                each = n_gy // len(blocks)
                groups.append([mine * n_gy + block * each + part for block in blocks for part in range(each)])
    return groups


def against(columns, rows):
    return lax.dot_general(
        columns, rows, (((0,), (0,)), ((), ())), preferred_element_type=jnp.float32, precision=lax.Precision.HIGH
    )


def section(state, register, checkpoint, velocity, diffusivity):
    nv, nz, ny, nx = state.shape
    to_yzx = lambda a: jnp.swapaxes(a, -3, -2)
    s, r, c = to_yzx(state), to_yzx(register), to_yzx(checkpoint)
    ylo, yhi, xlo, xhi = pack(s)
    up = lambda n: [(i, (i + 1) % n) for i in range(n)]
    down = lambda n: [(b, a) for a, b in up(n)]
    n_gx, n_gy = lax.axis_size("gx"), lax.axis_size("gy")
    xleft = lax.ppermute(xhi, "gx", up(n_gx))
    xright = lax.ppermute(xlo, "gx", down(n_gx))
    ybelow = lax.ppermute(yhi, "gy", up(n_gy))
    yabove = lax.ppermute(ylo, "gy", down(n_gy))
    new_state, new_register, change = stencil(
        s, r, c, to_yzx(velocity), to_yzx(diffusivity), ybelow, yabove, xleft, xright
    )
    depth = nv * ny * nz
    half = depth // 2
    mine = change.reshape(depth, nx)
    right = fetch(mine, 1, 0, 0)
    left = fetch(mine, -1, 0, 0)
    across = fetch(mine, 0, 1, 0)
    mine_c = fetch(mine, 0, 0, 1)
    far0 = fetch(right[:half], 1, 0, 0)
    far1 = fetch(left[half:], -1, 0, 0)
    right_c = fetch(right, 0, 0, 1)
    left_c = fetch(left, 0, 0, 1)
    far = jnp.pad(far0, ((0, half), (0, 0))) + jnp.pad(far1, ((half, 0), (0, 0)))
    far_c = fetch(far, 0, 0, 1)
    rows = jnp.concatenate([mine, across], axis=1)

    def products(*columns):
        return jnp.stack([against(a, rows) for a in columns])

    first = products(mine, mine_c, right, left, right_c, left_c)
    second = products(far, far_c)
    first_y = fetch(first[:, :, nx:], 0, 1, 0)
    second_y = fetch(second[:, :, nx:], 0, 1, 0)
    partial = jnp.concatenate([first[:, :, :nx], second[:, :, :nx], first_y, second_y], axis=0)
    partial = partial.reshape(n_gy, -1, nx)
    pieces = lax.all_to_all(partial, ("gx", "gy"), 0, 0, tiled=True, axis_index_groups=owners(n_gy))
    columns = nv * nz * ny * n_gy
    gram = jnp.sum(pieces, axis=0) / jnp.float32(columns)
    return to_yzx(new_state), to_yzx(new_register), gram.T


def solution(mesh):
    in_specs = (
        P(None, None, "gy", "gx"),
        P(None, None, "gy", "gx"),
        P(None, None, "gy", "gx"),
        P(None, None, "gy", "gx"),
        P(None, "gy", "gx"),
    )
    out_specs = (P(None, None, "gy", "gx"), P(None, None, "gy", "gx"), P("gx", "gy"))
    return jax.shard_map(section, mesh=mesh, in_specs=in_specs, out_specs=out_specs, check_vma=False)
```

```python
import jax
import jax.numpy as jnp
from jax import lax
from jax.experimental import pallas as pl
from jax.experimental.pallas import tpu as pltpu
from jax.sharding import PartitionSpec as P


step_size = 0.3
carry_weight = -5.0 / 9.0
update_weight = 15.0 / 16.0

NX_CHIPS, NY_LO, CORES = 4, 2, 2
HIGHEST = lax.Precision.HIGHEST
COLUMNS = (0, 1, 3, 2)
ROWS = ((0, 0), (0, 1), (1, 0), (1, 1))
FLIPS = (0, 2, 5, 6)


def gx_of(x, y, core):
    return (x % NX_CHIPS) * NY_LO * CORES + (y % NY_LO) * CORES + core % CORES


def from_offset(dx, dy, dcore):
    return [
        (gx_of(x + dx, y + dy, core + dcore), gx_of(x, y, core))
        for x in range(NX_CHIPS)
        for y in range(NY_LO)
        for core in range(CORES)
    ]


def fetch(value, dx, dy, dcore):
    return lax.ppermute(value, "gx", from_offset(dx, dy, dcore))


def edge_lanes():
    row = lax.broadcasted_iota(jnp.int32, (8, 128), 0)
    lane = lax.broadcasted_iota(jnp.int32, (8, 128), 1)
    wanted = jnp.where(row < 2, row, row + 124)
    return jnp.where((row < 4) & (lane == wanted), 1.0, 0.0).astype(jnp.float32)


def pack_kernel(s_ref, ylo_ref, yhi_ref, xlo_ref, xhi_ref):
    ny = s_ref.shape[1]
    ylo_ref[...] = s_ref[:, 0:2]
    yhi_ref[...] = s_ref[:, ny - 2 : ny]
    flat = s_ref[...].reshape(-1, 128)
    for start in range(0, flat.shape[0], 128):
        turned = flat[start : start + 128].T
        xlo_ref[:, start : start + 128] = turned[0:2]
        xhi_ref[:, start : start + 128] = turned[126:128]


def pack(s):
    nv, ny, nz, nx = s.shape
    f32 = jnp.float32
    return pl.pallas_call(
        pack_kernel,
        out_shape=(
            jax.ShapeDtypeStruct((nv, 2, nz, nx), f32),
            jax.ShapeDtypeStruct((nv, 2, nz, nx), f32),
            jax.ShapeDtypeStruct((2, nv * ny * nz), f32),
            jax.ShapeDtypeStruct((2, nv * ny * nz), f32),
        ),
        name="pack_edges",
    )(s)


def stencil_kernel(
    s_ref, r_ref, c_ref, vel_ref, dif_ref, ybelow_ref, yabove_ref, xleft_ref, xright_ref,
    ns_ref, nr_ref, chg_ref, halo_ref, edge_ref,
):
    nvb, ny, nz, nx = s_ref.shape
    halo_ref[...] = jnp.zeros_like(halo_ref)
    halo_ref[0:2, :] = xright_ref[...]
    halo_ref[2:4, :] = xleft_ref[...]
    edge_ref[...] = lax.dot_general(
        halo_ref[...], edge_lanes(), (((0,), (0,)), ((), ())), preferred_element_type=jnp.float32, precision=HIGHEST
    )
    lane = lax.broadcasted_iota(jnp.int32, (nz, nx), 1)

    def row(v, y):
        if y < 0:
            return ybelow_ref[v, y + 2]
        if y >= ny:
            return yabove_ref[v, y - ny]
        return s_ref[v, y]

    for v in range(nvb):
        for y in range(ny):
            f = row(v, y)
            e = edge_ref[pl.ds((v * ny + y) * nz, nz), :]
            xp1 = pltpu.roll(jnp.where(lane < 1, e, f), nx - 1, 1)
            xp2 = pltpu.roll(jnp.where(lane < 2, e, f), nx - 2, 1)
            xm1 = pltpu.roll(jnp.where(lane >= nx - 1, e, f), 1, 1)
            xm2 = pltpu.roll(jnp.where(lane >= nx - 2, e, f), 2, 1)
            yp1, yp2, ym1, ym2 = row(v, y + 1), row(v, y + 2), row(v, y - 1), row(v, y - 2)
            zp1 = pltpu.roll(f, nz - 1, 0)
            zp2 = pltpu.roll(f, nz - 2, 0)
            zm1 = pltpu.roll(f, 1, 0)
            zm2 = pltpu.roll(f, 2, 0)
            first_x = 8.0 * (xp1 - xm1) - (xp2 - xm2)
            first_y = 8.0 * (yp1 - ym1) - (yp2 - ym2)
            first_z = 8.0 * (zp1 - zm1) - (zp2 - zm2)
            near = (xp1 + xm1) + (yp1 + ym1) + (zp1 + zm1)
            far = (xp2 + xm2) + (yp2 + ym2) + (zp2 + zm2)
            spread = 16.0 * near - far - 90.0 * f
            advect = vel_ref[0, y] * first_x + vel_ref[1, y] * first_y + vel_ref[2, y] * first_z
            tendency = dif_ref[y] * spread - advect
            new_register = carry_weight * r_ref[v, y] + (step_size / 12.0) * tendency
            new_state = f + update_weight * new_register
            ns_ref[v, y] = new_state
            nr_ref[v, y] = new_register
            chg_ref[v, y] = new_state - c_ref[v, y].astype(jnp.float32)


def stencil(s, r, c, vel, dif, ybelow, yabove, xleft, xright, per_step=4):
    nv, ny, nz, nx = s.shape
    whole = pl.BlockSpec((per_step, ny, nz, nx), lambda i: (i, 0, 0, 0))
    side = pl.BlockSpec((per_step, 2, nz, nx), lambda i: (i, 0, 0, 0))
    cols = per_step * ny * nz
    edge = pl.BlockSpec((2, cols), lambda i: (0, i))
    out = jax.ShapeDtypeStruct(s.shape, jnp.float32)
    return pl.pallas_call(
        stencil_kernel,
        grid=(nv // per_step,),
        in_specs=[
            whole, whole, whole,
            pl.BlockSpec(vel.shape, lambda i: (0, 0, 0, 0)),
            pl.BlockSpec(dif.shape, lambda i: (0, 0, 0)),
            side, side, edge, edge,
        ],
        out_specs=[whole, whole, whole],
        out_shape=[out, out, out],
        scratch_shapes=[pltpu.VMEM((8, cols), jnp.float32), pltpu.VMEM((cols, nx), jnp.float32)],
        name="stencil",
    )(s, r, c, vel, dif, ybelow, yabove, xleft, xright)


def chips():
    return [(x, y, core) for x in range(NX_CHIPS) for y in range(NY_LO) for core in range(CORES)]


def slot(y, core):
    return y * 2 * CORES + core * 2


def reducers(n_gy):
    nz = n_gy // NX_CHIPS
    return [
        [
            gx_of(x, y, core) * n_gy + ((x + dx) % NX_CHIPS) * nz + ((slot(y, core) + part) ^ flip)
            for flip in FLIPS
            for dx in COLUMNS
            for part in range(2)
        ]
        for x, y, core in chips()
    ]


def to_owners(n_gy):
    nz = n_gy // NX_CHIPS
    return [
        (
            gx_of(x, y, core) * n_gy + block * nz + ((slot(y, core) + part) ^ flip),
            gx_of(x, y + dy, core + dcore) * n_gy + block * nz + slot(y, core) + part,
        )
        for x, y, core in chips()
        for (dy, dcore), flip in zip(ROWS[1:], FLIPS[1:])
        for block in range(NX_CHIPS)
        for part in range(2)
    ]


def against(columns, rows):
    return lax.dot_general(
        columns, rows, (((0,), (0,)), ((), ())), preferred_element_type=jnp.float32, precision=lax.Precision.HIGH
    )


def section(state, register, checkpoint, velocity, diffusivity):
    nv, nz, ny, nx = state.shape
    to_yzx = lambda a: jnp.swapaxes(a, -3, -2)
    s, r, c = to_yzx(state), to_yzx(register), to_yzx(checkpoint)
    ylo, yhi, xlo, xhi = pack(s)
    up = lambda n: [(i, (i + 1) % n) for i in range(n)]
    down = lambda n: [(b, a) for a, b in up(n)]
    n_gx, n_gy = lax.axis_size("gx"), lax.axis_size("gy")
    xleft = lax.ppermute(xhi, "gx", up(n_gx))
    xright = lax.ppermute(xlo, "gx", down(n_gx))
    ybelow = lax.ppermute(yhi, "gy", up(n_gy))
    yabove = lax.ppermute(ylo, "gy", down(n_gy))
    new_state, new_register, change = stencil(
        s, r, c, to_yzx(velocity), to_yzx(diffusivity), ybelow, yabove, xleft, xright
    )
    depth = nv * ny * nz
    half = depth // 2
    mine = change.reshape(depth, nx)
    right = fetch(mine, 1, 0, 0)
    left = fetch(mine, -1, 0, 0)
    across = fetch(mine, 0, 1, 0)
    mine_c = fetch(mine, 0, 0, 1)
    far0 = fetch(right[:half], 1, 0, 0)
    far1 = fetch(left[half:], -1, 0, 0)
    across_c = fetch(across, 0, 0, 1)
    row_pairs = [jnp.concatenate(pair, axis=1) for pair in ((mine, mine_c), (across, across_c))]

    def products(rows):
        near = [against(a, rows) for a in (mine, right, left)]
        return jnp.stack(near + [against(far0, rows[:half]) + against(far1, rows[half:])])

    parts = [products(rows) for rows in row_pairs]
    partial = jnp.concatenate([p[:, :, lanes] for p in parts for lanes in (slice(0, nx), slice(nx, 2 * nx))], axis=0)
    partial = partial.reshape(n_gy, -1, nx)
    both = ("gx", "gy")
    pieces = lax.all_to_all(partial, both, 0, 0, tiled=True, axis_index_groups=reducers(n_gy))
    summed = jnp.sum(pieces, axis=0)
    moved = lax.ppermute(summed, both, to_owners(n_gy))
    gx, z = lax.axis_index("gx"), lax.rem(lax.axis_index("gy"), n_gy // NX_CHIPS)
    stays = lax.div(z, 2) == lax.rem(gx, NY_LO * CORES)
    columns = nv * nz * ny * n_gy
    gram = jnp.where(stays, summed, moved) / jnp.float32(columns)
    return to_yzx(new_state), to_yzx(new_register), gram.T


def solution(mesh):
    in_specs = (
        P(None, None, "gy", "gx"),
        P(None, None, "gy", "gx"),
        P(None, None, "gy", "gx"),
        P(None, None, "gy", "gx"),
        P(None, "gy", "gx"),
    )
    out_specs = (P(None, None, "gy", "gx"), P(None, None, "gy", "gx"), P("gx", "gy"))
    return jax.shard_map(
        section, mesh=mesh, in_specs=in_specs, out_specs=out_specs, check_vma=False
    )
```

```python
import jax
import jax.numpy as jnp
from jax import lax
from jax.experimental import pallas as pl
from jax.experimental.pallas import tpu as pltpu
from jax.sharding import PartitionSpec as P


step_size = 0.3
carry_weight = -5.0 / 9.0
update_weight = 15.0 / 16.0

NX_CHIPS, NY_LO, CORES = 4, 2, 2
HIGHEST = lax.Precision.HIGHEST
COLUMNS = (0, 1, 3, 2)
ROWS = ((0, 0), (0, 1), (1, 0), (1, 1))
FLIPS = (0, 2, 5, 6)


def gx_of(x, y, core):
    return (x % NX_CHIPS) * NY_LO * CORES + (y % NY_LO) * CORES + core % CORES


def from_offset(dx, dy, dcore):
    return [
        (gx_of(x + dx, y + dy, core + dcore), gx_of(x, y, core))
        for x in range(NX_CHIPS)
        for y in range(NY_LO)
        for core in range(CORES)
    ]


def fetch(value, dx, dy, dcore):
    return lax.ppermute(value, "gx", from_offset(dx, dy, dcore))


def edge_lanes():
    row = lax.broadcasted_iota(jnp.int32, (8, 128), 0)
    lane = lax.broadcasted_iota(jnp.int32, (8, 128), 1)
    wanted = jnp.where(row < 2, row, row + 124)
    return jnp.where((row < 4) & (lane == wanted), 1.0, 0.0).astype(jnp.float32)


def pack_kernel(s_ref, ylo_ref, yhi_ref, xlo_ref, xhi_ref):
    ny = s_ref.shape[1]
    ylo_ref[...] = s_ref[:, 0:2]
    yhi_ref[...] = s_ref[:, ny - 2 : ny]
    flat = s_ref[...].reshape(-1, 128)
    for start in range(0, flat.shape[0], 128):
        turned = flat[start : start + 128].T
        xlo_ref[:, start : start + 128] = turned[0:2]
        xhi_ref[:, start : start + 128] = turned[126:128]


def pack(s):
    nv, ny, nz, nx = s.shape
    f32 = jnp.float32
    return pl.pallas_call(
        pack_kernel,
        out_shape=(
            jax.ShapeDtypeStruct((nv, 2, nz, nx), f32),
            jax.ShapeDtypeStruct((nv, 2, nz, nx), f32),
            jax.ShapeDtypeStruct((2, nv * ny * nz), f32),
            jax.ShapeDtypeStruct((2, nv * ny * nz), f32),
        ),
        name="pack_edges",
    )(s)


def stencil_kernel(
    s_ref, r_ref, c_ref, vel_ref, dif_ref, ybelow_ref, yabove_ref, xleft_ref, xright_ref,
    ns_ref, nr_ref, chg_ref, front_ref, back_ref, halo_ref, edge_ref,
):
    nvb, ny, nz, nx = s_ref.shape
    halo_ref[...] = jnp.zeros_like(halo_ref)
    halo_ref[0:2, :] = xright_ref[...]
    halo_ref[2:4, :] = xleft_ref[...]
    edge_ref[...] = lax.dot_general(
        halo_ref[...], edge_lanes(), (((0,), (0,)), ((), ())), preferred_element_type=jnp.float32, precision=HIGHEST
    )
    lane = lax.broadcasted_iota(jnp.int32, (nz, nx), 1)

    def row(v, y):
        if y < 0:
            return ybelow_ref[v, y + 2]
        if y >= ny:
            return yabove_ref[v, y - ny]
        return s_ref[v, y]

    for v in range(nvb):
        for y in range(ny):
            f = row(v, y)
            e = edge_ref[pl.ds((v * ny + y) * nz, nz), :]
            xp1 = pltpu.roll(jnp.where(lane < 1, e, f), nx - 1, 1)
            xp2 = pltpu.roll(jnp.where(lane < 2, e, f), nx - 2, 1)
            xm1 = pltpu.roll(jnp.where(lane >= nx - 1, e, f), 1, 1)
            xm2 = pltpu.roll(jnp.where(lane >= nx - 2, e, f), 2, 1)
            yp1, yp2, ym1, ym2 = row(v, y + 1), row(v, y + 2), row(v, y - 1), row(v, y - 2)
            zp1 = pltpu.roll(f, nz - 1, 0)
            zp2 = pltpu.roll(f, nz - 2, 0)
            zm1 = pltpu.roll(f, 1, 0)
            zm2 = pltpu.roll(f, 2, 0)
            first_x = 8.0 * (xp1 - xm1) - (xp2 - xm2)
            first_y = 8.0 * (yp1 - ym1) - (yp2 - ym2)
            first_z = 8.0 * (zp1 - zm1) - (zp2 - zm2)
            near = (xp1 + xm1) + (yp1 + ym1) + (zp1 + zm1)
            far = (xp2 + xm2) + (yp2 + ym2) + (zp2 + zm2)
            spread = 16.0 * near - far - 90.0 * f
            advect = vel_ref[0, y] * first_x + vel_ref[1, y] * first_y + vel_ref[2, y] * first_z
            tendency = dif_ref[y] * spread - advect
            new_register = carry_weight * r_ref[v, y] + (step_size / 12.0) * tendency
            new_state = f + update_weight * new_register
            ns_ref[v, y] = new_state
            nr_ref[v, y] = new_register
            chg_ref[v, y] = new_state - c_ref[v, y].astype(jnp.float32)

    @pl.when(pl.program_id(0) == 0)
    def _():
        front_ref[...] = chg_ref[...]

    @pl.when(pl.program_id(0) == 1)
    def _():
        back_ref[...] = chg_ref[...]


def stencil(s, r, c, vel, dif, ybelow, yabove, xleft, xright):
    nv, ny, nz, nx = s.shape
    per_step = nv // 2
    whole = pl.BlockSpec((per_step, ny, nz, nx), lambda i: (i, 0, 0, 0))
    side = pl.BlockSpec((per_step, 2, nz, nx), lambda i: (i, 0, 0, 0))
    cols = per_step * ny * nz
    edge = pl.BlockSpec((2, cols), lambda i: (0, i))
    out = jax.ShapeDtypeStruct(s.shape, jnp.float32)
    half = jax.ShapeDtypeStruct((per_step, ny, nz, nx), jnp.float32)
    part = pl.BlockSpec(half.shape, lambda i: (0, 0, 0, 0))
    return pl.pallas_call(
        stencil_kernel,
        grid=(nv // per_step,),
        in_specs=[
            whole, whole, whole,
            pl.BlockSpec(vel.shape, lambda i: (0, 0, 0, 0)),
            pl.BlockSpec(dif.shape, lambda i: (0, 0, 0)),
            side, side, edge, edge,
        ],
        out_specs=[whole, whole, whole, part, part],
        out_shape=[out, out, out, half, half],
        scratch_shapes=[pltpu.VMEM((8, cols), jnp.float32), pltpu.VMEM((cols, nx), jnp.float32)],
        name="stencil",
    )(s, r, c, vel, dif, ybelow, yabove, xleft, xright)


def chips():
    return [(x, y, core) for x in range(NX_CHIPS) for y in range(NY_LO) for core in range(CORES)]


def slot(y, core):
    return y * 2 * CORES + core * 2


def reducers(n_gy):
    nz = n_gy // NX_CHIPS
    return [
        [
            gx_of(x, y, core) * n_gy + ((x + dx) % NX_CHIPS) * nz + ((slot(y, core) + part) ^ flip)
            for flip in FLIPS
            for dx in COLUMNS
            for part in range(2)
        ]
        for x, y, core in chips()
    ]


def to_owners(n_gy):
    nz = n_gy // NX_CHIPS
    return [
        (
            gx_of(x, y, core) * n_gy + block * nz + ((slot(y, core) + part) ^ flip),
            gx_of(x, y + dy, core + dcore) * n_gy + block * nz + slot(y, core) + part,
        )
        for x, y, core in chips()
        for (dy, dcore), flip in zip(ROWS[1:], FLIPS[1:])
        for block in range(NX_CHIPS)
        for part in range(2)
    ]


def against(columns, rows):
    return lax.dot_general(
        columns, rows, (((0,), (0,)), ((), ())), preferred_element_type=jnp.float32, precision=lax.Precision.HIGH
    )


def section(state, register, checkpoint, velocity, diffusivity):
    nv, nz, ny, nx = state.shape
    to_yzx = lambda a: jnp.swapaxes(a, -3, -2)
    s, r, c = to_yzx(state), to_yzx(register), to_yzx(checkpoint)
    ylo, yhi, xlo, xhi = pack(s)
    up = lambda n: [(i, (i + 1) % n) for i in range(n)]
    down = lambda n: [(b, a) for a, b in up(n)]
    n_gx, n_gy = lax.axis_size("gx"), lax.axis_size("gy")
    xleft = lax.ppermute(xhi, "gx", up(n_gx))
    xright = lax.ppermute(xlo, "gx", down(n_gx))
    ybelow = lax.ppermute(yhi, "gy", up(n_gy))
    yabove = lax.ppermute(ylo, "gy", down(n_gy))
    new_state, new_register, change, front, back = stencil(
        s, r, c, to_yzx(velocity), to_yzx(diffusivity), ybelow, yabove, xleft, xright
    )
    depth = nv * ny * nz
    half = depth // 2
    mine = change.reshape(depth, nx)
    front, back = front.reshape(half, nx), back.reshape(half, nx)
    right0 = fetch(front, 1, 0, 0)
    left1 = fetch(back, -1, 0, 0)
    across = fetch(mine, 0, 1, 0)
    right1 = fetch(back, 1, 0, 0)
    left0 = fetch(front, -1, 0, 0)
    far0 = fetch(right0, 1, 0, 0)
    far1 = fetch(left1, -1, 0, 0)
    mine_c = fetch(mine, 0, 0, 1)
    across_c = fetch(across, 0, 0, 1)
    row_pairs = [jnp.concatenate(pair, axis=1) for pair in ((mine, mine_c), (across, across_c))]

    def products(rows):
        def by_halves(a, b):
            return against(a, rows[:half]) + against(b, rows[half:])

        near = [against(mine, rows), by_halves(right0, right1), by_halves(left0, left1)]
        return jnp.stack(near + [by_halves(far0, far1)])

    parts = [products(rows) for rows in row_pairs]
    partial = jnp.concatenate([p[:, :, lanes] for p in parts for lanes in (slice(0, nx), slice(nx, 2 * nx))], axis=0)
    partial = partial.reshape(n_gy, -1, nx)
    both = ("gx", "gy")
    pieces = lax.all_to_all(partial, both, 0, 0, tiled=True, axis_index_groups=reducers(n_gy))
    summed = jnp.sum(pieces, axis=0)
    moved = lax.ppermute(summed, both, to_owners(n_gy))
    gx, z = lax.axis_index("gx"), lax.rem(lax.axis_index("gy"), n_gy // NX_CHIPS)
    stays = lax.div(z, 2) == lax.rem(gx, NY_LO * CORES)
    columns = nv * nz * ny * n_gy
    gram = jnp.where(stays, summed, moved) / jnp.float32(columns)
    return to_yzx(new_state), to_yzx(new_register), gram.T


def solution(mesh):
    in_specs = (
        P(None, None, "gy", "gx"),
        P(None, None, "gy", "gx"),
        P(None, None, "gy", "gx"),
        P(None, None, "gy", "gx"),
        P(None, "gy", "gx"),
    )
    out_specs = (P(None, None, "gy", "gx"), P(None, None, "gy", "gx"), P("gx", "gy"))
    return jax.shard_map(
        section, mesh=mesh, in_specs=in_specs, out_specs=out_specs, check_vma=False
    )
```
